32 devices in a mesh: tm: 8 (over z, y), space: 4 (over x, core).
Axes of the slice: x: 2, y: 2, z: 4, core: 2. Of those that a mesh axis runs over, the one named last changes fastest.
Arguments:
- initial_guess: float32 [8, 1024, 1024], P('tm', 'space'), may hold values from -6 to 6
- start_field: float32 [1024, 1024], P('space'), may hold values from -6 to 6
- source_field: float32 [1024, 1024], P('space'), may hold values from -0.3 to 0.3
Outputs:
- final_states: float32 [8, 1024, 1024], P('tm', 'space')
The draws below stay inside these ranges and needn't reach their ends.
All inputs are finite; a program needn't handle non-finite values.
Results may differ from the reference program's by a relative error of at most 0.00013.
Values sent between devices are 32-bit elements; how exact they have to be, the bound alone decides.
A program may use at most 64 MiB of HBM per device.

```python
import jax
import jax.numpy as jnp
from jax import lax

N = 1024
M = 16
ITERS = 1
K = 8


def levels(key, extent, split, smallest, high):
    factor_of = 1.0
    for position, shards_of in split:
        heights = jax.random.uniform(jax.random.fold_in(jax.random.fold_in(key, 6), position), (shards_of,), jnp.float32, smallest / len(split), high / len(split))
        factor_of = factor_of * jnp.repeat(jnp.exp(heights), extent[position] // shards_of).reshape((-1,) + (1,) * (len(extent) - 1 - position))
    return factor_of


def centred(own_key, shape, deviation, bound, shards=(), held_as=jnp.bfloat16):
    entries = deviation * jax.random.normal(own_key, shape, jnp.float32)
    if shards:
        entries = entries * levels(own_key, shape, shards, -0.22, 0.18)
    return jnp.clip(entries, -bound, bound).astype(held_as)


def setup_inputs(seed: int = 0) -> dict:
    arg_keys = jax.random.split(jax.random.key(seed), 4)
    return {
        "initial_guess": centred(arg_keys[0], (K, N, N), 1.0, 6.0, ((0, 8), (1, 4)), jnp.float32),
        "start_field": centred(arg_keys[1], (N, N), 1.0, 6.0, ((0, 4),), jnp.float32),
        "source_field": centred(arg_keys[2], (N, N), 0.05, 0.3, ((0, 4),), jnp.float32),
    }


decay_rate = 0.0005
spread_rate = 0.01


def mode_symbols():
    mode_index = jnp.arange(N).astype(jnp.float32)
    half_sines = jnp.sin(jnp.pi * mode_index / N) ** 2
    stiffness = 4.0 * (half_sines[:, None] + half_sines[None, :])
    fine_factor = 1.0 / (1.0 + decay_rate + spread_rate * stiffness)
    coarse_factor = 1.0 / (1.0 + M * decay_rate + M * spread_rate * stiffness)
    fine_power = jnp.ones_like(fine_factor)
    forcing_symbol = jnp.zeros_like(fine_factor)
    for substep in range(M):
        fine_power = fine_power * fine_factor
        forcing_symbol = forcing_symbol + fine_power
    return fine_power, forcing_symbol, coarse_factor


def propagate(symbol, fields):
    return jnp.real(jnp.fft.ifft2(symbol * jnp.fft.fft2(fields))).astype(jnp.float32)


def reference(initial_guess, start_field, source_field):
    fine_power, forcing_symbol, coarse_factor = mode_symbols()
    forcing = propagate(forcing_symbol, source_field)
    states = initial_guess
    for iteration in range(ITERS):
        previous = jnp.concatenate([start_field[None], states[:-1]], axis=0)
        relaxed = propagate(fine_power, previous) + forcing
        previous_relaxed = jnp.concatenate([start_field[None], relaxed[:-1]], axis=0)
        residual = propagate(fine_power, previous_relaxed) + forcing - relaxed
        residual_hat = jnp.fft.fft2(residual)

        def advance(carried, current):
            updated = coarse_factor * carried + current
            return updated, updated

        unused, errors_hat = lax.scan(advance, jnp.zeros_like(residual_hat[0]), residual_hat)
        states = relaxed + jnp.real(jnp.fft.ifft2(errors_hat)).astype(jnp.float32)
    return states
```

```python
import functools

import jax
import jax.numpy as jnp
import numpy as np
from jax import lax
from jax.experimental import pallas as pl
from jax.experimental.pallas import tpu as pltpu
from jax.sharding import PartitionSpec as P

M = 16
MESH = pl.DeviceIdType.MESH

decay_rate = 0.0005
spread_rate = 0.01


def mode_order(length):
    return np.concatenate([np.arange(0, length, 2), np.arange(1, length, 2)])


def half_kernels(length):
    half = length // 2
    product = mode_order(length)[:, None] * np.arange(half)[None, :] % length
    angles = 2.0 * np.pi / length * product
    full = (np.cos(angles) + np.sin(angles)).astype(np.float32).reshape(2, half, half)
    high = full.astype(jnp.bfloat16)
    low = (full - high.astype(np.float32)).astype(jnp.bfloat16)
    return np.stack([high, low])


def split(value):
    high = value.astype(jnp.bfloat16)
    low = (value - high.astype(jnp.float32)).astype(jnp.bfloat16)
    return high, low


def dot(a, b):
    return lax.dot_general(a, b, (((1,), (0,)), ((), ())), preferred_element_type=jnp.float32)


def dot3(a_high, a_low, b_high, b_low):
    rows = a_high.shape[0]
    both = dot(jnp.concatenate([a_high, a_low], axis=0), b_high)
    return both[:rows] + (both[rows:] + dot(a_high, b_low))


def mgrit_kernel(
    turns, shards, planes, chunks, lag, slope, late,
    guess, start, source, kernels_hbm, turned_hbm, rows_hbm, columns_hbm, out_ref,
    field, extra, kernels, turned, row_sines, column_sines, field_high, field_low, extra_high, extra_low,
    along, along_extra, gathered, spectra, states, crossing, spread, returned, total,
    load_sem, kernel_sem, turned_sem, rows_sem, columns_sem, send_one, recv_one, send_extra, send_start,
    send_cross, recv_cross, send_two, recv_two,
):
    tm, space = lax.axis_index("tm"), lax.axis_index("space")
    width = turns // planes
    group = width * shards
    last = planes - 1
    plane = tm // width
    place = lax.rem(tm, width)
    me = place * shards + space
    rows, length = field.shape
    half = length // 2
    tile = length // chunks
    deep = tile // group
    per_parity = chunks // 2
    has_guess = tm < turns - 2
    sourced = plane < (planes if width > 2 else last)
    wait_for = lag + slope * plane

    field_load = pltpu.make_async_copy(guess.at[0], field, load_sem.at[0])
    field_load.start()
    kernel_load = pltpu.make_async_copy(kernels_hbm, kernels, kernel_sem)
    kernel_load.start()
    turned_load = pltpu.make_async_copy(turned_hbm, turned, turned_sem)
    turned_load.start()
    source_load = pltpu.make_async_copy(source, extra.at[pl.ds(0, rows), :], load_sem.at[1])
    source_load.start()
    start_load = pltpu.make_async_copy(start, extra.at[pl.ds(rows, rows), :], load_sem.at[2])
    start_load.start()
    columns_load = pltpu.make_async_copy(columns_hbm, column_sines, columns_sem)
    columns_load.start()

    def rows_load(chunk):
        return pltpu.make_async_copy(
            rows_hbm.at[pl.ds(pl.multiple_of(chunk * tile + me * deep, deep), deep), :],
            row_sines.at[pl.ds(pl.multiple_of(chunk * deep, deep), deep), :], rows_sem)

    for chunk in range(chunks):
        rows_load(chunk).start()

    def device(where, peer):
        return (where * width + peer // shards, lax.rem(peer, shards))

    def every(count, act):
        def turn(step, carry):
            act(step)
            return carry

        lax.fori_loop(0, count, turn, 0)

    def around(mine, count, act):
        def turn(step, carry):
            act(lax.rem(mine + step, count))
            return carry

        lax.fori_loop(1, count, turn, 0)

    barrier = pltpu.get_barrier_semaphore()

    def greet(who):
        pl.semaphore_signal(barrier, inc=1, device_id=who, device_id_type=MESH)

    around(me, group, lambda peer: greet(device(plane, peer)))

    @pl.when(plane > 0)
    def _():
        greet((tm - width, space))

    @pl.when(plane == 0)
    def _():
        every(shards, lambda shard: greet((last * width + place, shard)))

    def rows_of(base, index):
        return pl.ds(pl.multiple_of(base + index * deep, deep), deep)

    def first_copy(chunk, peer):
        return pltpu.make_async_remote_copy(
            src_ref=along.at[rows_of(chunk * tile, peer), :],
            dst_ref=gathered.at[chunk, space, rows_of(0, place), :],
            send_sem=send_one, recv_sem=recv_one.at[chunk],
            device_id=device(plane, peer), device_id_type=MESH)

    def first_own(chunk):
        return pltpu.make_async_copy(
            along.at[rows_of(chunk * tile, me), :], gathered.at[chunk, space, rows_of(0, place), :],
            recv_one.at[chunk])

    def source_copy(chunk, shard):
        return pltpu.make_async_remote_copy(
            src_ref=along_extra.at[chunk, 0, rows_of(0, shard), :],
            dst_ref=gathered.at[chunk, space, pl.ds(width * deep, deep), :],
            send_sem=send_extra, recv_sem=recv_one.at[chunk],
            device_id=(tm, shard), device_id_type=MESH)

    def source_own(chunk):
        return pltpu.make_async_copy(
            along_extra.at[chunk, 0, rows_of(0, space), :], gathered.at[chunk, space, pl.ds(width * deep, deep), :],
            recv_one.at[chunk])

    def start_copy(chunk, shard):
        return pltpu.make_async_remote_copy(
            src_ref=along_extra.at[chunk, 1, rows_of(0, shard), :],
            dst_ref=gathered.at[chunk, space, pl.ds((width + 1) * deep, deep), :],
            send_sem=send_start, recv_sem=recv_one.at[chunk],
            device_id=(place, shard), device_id_type=MESH)

    def cross_copy(chunk):
        return pltpu.make_async_remote_copy(
            src_ref=crossing.at[chunk], dst_ref=states.at[chunk, pl.ds(0, 2 * deep), :],
            send_sem=send_cross, recv_sem=recv_cross.at[chunk],
            device_id=(tm + width, space), device_id_type=MESH)

    def second_copy(chunk, peer):
        return pltpu.make_async_remote_copy(
            src_ref=spread.at[chunk, lax.rem(peer, shards), rows_of(0, peer // shards), :],
            dst_ref=returned.at[rows_of(chunk * tile, me), :],
            send_sem=send_two, recv_sem=recv_two.at[chunk],
            device_id=device(plane, peer), device_id_type=MESH)

    def second_own(chunk):
        return pltpu.make_async_copy(
            spread.at[chunk, space, rows_of(0, place), :], returned.at[rows_of(chunk * tile, me), :],
            recv_two.at[chunk])

    def arrived(ref, sem):
        pltpu.make_async_copy(ref, ref, sem).wait()

    def fold(value, high_ref, low_ref, columns):
        first, second = value[:, :half], value[:, half:]
        for which, part in enumerate((first + second, first - second)):
            high_ref[which, :, columns], low_ref[which, :, columns] = split(part.T)

    field_load.wait()
    fold(field[...], field_high, field_low, slice(0, rows))
    source_load.wait()
    fold(extra[:rows], extra_high, extra_low, slice(0, rows))
    start_load.wait()

    @pl.when(plane == last)
    def _():
        fold(extra[rows:], extra_high, extra_low, slice(rows, 2 * rows))

    kernel_load.wait()
    pl.semaphore_wait(
        barrier,
        group - 1 + jnp.where(plane < last, 1, shards))

    def outward(chunk, carry):
        which = chunk // per_parity
        offset = lax.rem(chunk, per_parity) * tile

        @pl.when(has_guess)
        def _():
            part = pl.ds(pl.multiple_of(offset, tile), tile)
            along[pl.ds(pl.multiple_of(chunk * tile, tile), tile), :] = dot3(
                kernels[0, which, part, :], kernels[1, which, part, :], field_high[which], field_low[which])

            first_own(chunk).start()
            around(me, group, lambda peer: first_copy(chunk, peer).start())

        mine = pl.ds(pl.multiple_of(offset + place * (shards * deep), shards * deep), shards * deep)
        high, low = kernels[0, which, mine, :], kernels[1, which, mine, :]

        @pl.when(sourced)
        def _():
            along_extra[chunk, 0] = dot3(high, low, extra_high[which, :, :rows], extra_low[which, :, :rows])
            around(space, shards, lambda shard: source_copy(chunk, shard).start())
            source_own(chunk).start()

        @pl.when(plane == last)
        def _():
            along_extra[chunk, 1] = dot3(high, low, extra_high[which, :, rows:], extra_low[which, :, rows:])
            start_copy(chunk, space).start()
            around(space, shards, lambda shard: start_copy(chunk, shard).start())

        return carry

    lax.fori_loop(0, chunks, outward, 0)
    arrived(row_sines, rows_sem)
    columns_load.wait()
    turned_load.wait()
    total[...] = jnp.zeros_like(total)

    lanes = 256
    across = length // lanes
    scale = 1.0 / float(length * length)
    steps = deep // 8 * across

    def mix(chunk, kind, index, carry):
        row = pl.multiple_of(index // across * 8, 8)
        lane = pl.ds(pl.multiple_of(lax.rem(index, across) * lanes, lanes), lanes)
        sines = row_sines[pl.ds(pl.multiple_of(chunk * deep + row, 8), 8), :]
        stiffness = 4.0 * (column_sines[:, lane] + jnp.concatenate([sines] * (lanes // 128), axis=1))
        fine_factor = 1.0 / (1.0 + decay_rate + spread_rate * stiffness)
        coarse = 1.0 / (1.0 + M * decay_rate + M * spread_rate * stiffness)
        fine, symbol, power = fine_factor, fine_factor, 1
        while power < M:
            symbol = symbol + fine * symbol
            fine = fine * fine
            power *= 2

        def at(turn):
            return pl.ds(pl.multiple_of(turn * deep + row, 8), 8)

        forcing = symbol * (scale * spectra[chunk, at(width), lane])
        gain = (fine * scale) * (fine - coarse)
        source_gain = (1.0 + fine - coarse) * forcing
        if kind == "first":
            state = fine * (scale * spectra[chunk, at(width + 1), lane]) + forcing
            states[chunk, at(0), lane] = state
            state = fine * state + forcing
            states[chunk, at(1), lane] = state
        else:
            state = states[chunk, at(1), lane]
        for turn in range(2, width if kind == "last" else width + 2):
            state = coarse * state + (gain * spectra[chunk, at(turn - 2), lane] + source_gain)
            if turn < width:
                states[chunk, at(turn), lane] = state
            else:
                crossing[chunk, at(turn - width), lane] = state
        return carry

    def transform(chunk):
        for condition, count in ((plane == 0, width + 2), ((plane > 0) & (plane < last), width + 1), (plane == last, width - 1)):
            if width > 2 or count > 1:
                @pl.when(condition)
                def _():
                    arrived(gathered.at[chunk, :, pl.ds(0, count * deep), :], recv_one.at[chunk])

        upper = [gathered[chunk, shard] for shard in range(shards // 2)]
        lower = [gathered[chunk, shard + shards // 2] for shard in range(shards // 2)]
        sums = [jnp.concatenate([a + b for a, b in zip(upper, lower)], axis=1)]
        sums.append(jnp.concatenate([a - b for a, b in zip(upper, lower)], axis=1))
        for which in range(2):
            right = (kernels[0, 0], kernels[1, 0]) if which == 0 else (turned[0], turned[1])
            spectra[chunk, :, which * half:(which + 1) * half] = dot3(*split(sums[which]), *right)

        @pl.when(plane == 0)
        def _():
            lax.fori_loop(0, steps, functools.partial(mix, chunk, "first"), 0)
            cross_copy(chunk).start()

    def advance(chunk):
        @pl.when(plane > 0)
        def _():
            arrived(states.at[chunk, pl.ds(0, 2 * deep), :], recv_cross.at[chunk])

        @pl.when((plane > 0) & (plane < last))
        def _():
            lax.fori_loop(0, steps, functools.partial(mix, chunk, "middle"), 0)
            cross_copy(chunk).start()

        if width > 2:
            @pl.when(plane == last)
            def _():
                lax.fori_loop(0, steps, functools.partial(mix, chunk, "last"), 0)

        even_high, even_low = split(states[chunk, :, :half])
        odd_high, odd_low = split(states[chunk, :, half:])
        for shard in range(shards // 2):
            columns = slice(shard * rows, (shard + 1) * rows)
            even = dot3(even_high, even_low, kernels[0, 0, :, columns], kernels[1, 0, :, columns])
            odd = dot3(odd_high, odd_low, kernels[0, 1, :, columns], kernels[1, 1, :, columns])
            spread[chunk, shard] = even + odd
            spread[chunk, shard + shards // 2] = even - odd
        second_own(chunk).start()
        around(me, group, lambda peer: second_copy(chunk, peer).start())

    def inward(chunk):
        block = pl.ds(pl.multiple_of(chunk * tile, tile), tile)
        arrived(returned.at[block, :], recv_two.at[chunk])
        which = chunk // per_parity
        part = pl.ds(pl.multiple_of(lax.rem(chunk, per_parity) * tile, tile), tile)
        high, low = split(returned[block, :].T)
        total[which] += dot3(high, low, kernels[0, which, part, :], kernels[1, which, part, :])

    def step(time, carry):
        @pl.when((time < chunks) & sourced)
        def _():
            transform(time)

        @pl.when((time >= wait_for) & (time < wait_for + chunks))
        def _():
            advance(time - wait_for)

        @pl.when(time >= wait_for + late)
        def _():
            inward(time - wait_for - late)

        return carry

    lax.fori_loop(0, chunks + wait_for + late, step, 0)
    out_ref[0, :, :half] = total[0] + total[1]
    out_ref[0, :, half:] = total[0] - total[1]

    @pl.when(has_guess)
    def _():
        arrived(along.at[pl.ds(0, (group - 1) * deep * chunks), :], send_one)

    @pl.when(sourced)
    def _():
        arrived(along_extra.at[:, 0, pl.ds(0, (shards - 1) * deep), :], send_extra)

    @pl.when(plane == last)
    def _():
        arrived(along_extra.at[:, 1], send_start)

    @pl.when(plane < last)
    def _():
        arrived(crossing, send_cross)

    arrived(along.at[pl.ds(0, (group - 1) * deep * chunks), :], send_two)


def body(turns, shards, initial_guess, start_field, source_field):
    rows, length = start_field.shape
    planes = 2
    width = turns // planes
    group = width * shards
    half = length // 2
    chunks = min(8, length // group // 8)
    tile = length // chunks
    deep = tile // group
    halves = half_kernels(length)
    kernels = jnp.asarray(halves)
    turned = jnp.asarray(np.ascontiguousarray(halves[:, 1].transpose(0, 2, 1)))
    sines = (np.sin(np.pi * mode_order(length) / length) ** 2).astype(np.float32)
    row_sines = jnp.asarray(np.repeat(sines[:, None], 128, axis=1))
    column_sines = jnp.asarray(np.repeat(sines[None, :], 8, axis=0))
    f32, bf16 = jnp.float32, jnp.bfloat16
    dma = pltpu.SemaphoreType.DMA
    return pl.pallas_call(
        functools.partial(mgrit_kernel, turns, shards, planes, chunks, 1, 0, 8),
        out_shape=jax.ShapeDtypeStruct(initial_guess.shape, f32),
        in_specs=[pl.BlockSpec(memory_space=pltpu.HBM)] * 7,
        out_specs=pl.BlockSpec(memory_space=pltpu.VMEM),
        scratch_shapes=[
            pltpu.VMEM((rows, length), f32),
            pltpu.VMEM((2 * rows, length), f32),
            pltpu.VMEM((2, 2, half, half), bf16),
            pltpu.VMEM((2, half, half), bf16),
            pltpu.VMEM((chunks * deep, 128), f32),
            pltpu.VMEM((8, length), f32),
            pltpu.VMEM((2, half, rows), bf16),
            pltpu.VMEM((2, half, rows), bf16),
            pltpu.VMEM((2, half, 2 * rows), bf16),
            pltpu.VMEM((2, half, 2 * rows), bf16),
            pltpu.VMEM((length, rows), f32),
            pltpu.VMEM((chunks, 2, shards * deep, rows), f32),
            pltpu.VMEM((chunks, shards, (width + 2) * deep, rows), f32),
            pltpu.VMEM((chunks, (width + 2) * deep, length), f32),
            pltpu.VMEM((chunks, width * deep, length), f32),
            pltpu.VMEM((chunks, 2 * deep, length), f32),
            pltpu.VMEM((chunks, shards, width * deep, rows), f32),
            pltpu.VMEM((length, rows), f32),
            pltpu.VMEM((2, rows, half), f32),
            dma((3,)), dma, dma, dma, dma, dma, dma((chunks,)), dma, dma,
            dma, dma((chunks,)), dma, dma((chunks,)),
        ],
        compiler_params=pltpu.CompilerParams(
            collective_id=0, has_side_effects=True, vmem_limit_bytes=40 * 1024 * 1024),
    )(*(pltpu.with_memory_space_constraint(value, pltpu.HBM)
        for value in (initial_guess, start_field, source_field, kernels, turned, row_sines, column_sines)))


def solution(mesh):
    return jax.shard_map(
        functools.partial(body, mesh.shape["tm"], mesh.shape["space"]),
        mesh=mesh,
        in_specs=(P("tm", "space", None), P("space", None), P("space", None)),
        out_specs=P("tm", "space", None),
        check_vma=False,
    )
```

```python
import functools

import jax
import jax.numpy as jnp
import numpy as np
from jax import lax
from jax.experimental import pallas as pl
from jax.experimental.pallas import tpu as pltpu
from jax.sharding import PartitionSpec as P

M = 16
MESH = pl.DeviceIdType.MESH

decay_rate = 0.0005
spread_rate = 0.01


def mode_order(length):
    return np.concatenate([np.arange(0, length, 2), np.arange(1, length, 2)])


def half_kernels(length):
    half = length // 2
    product = mode_order(length)[:, None] * np.arange(half)[None, :] % length
    angles = 2.0 * np.pi / length * product
    full = (np.cos(angles) + np.sin(angles)).astype(np.float32).reshape(2, half, half)
    high = full.astype(jnp.bfloat16)
    low = (full - high.astype(np.float32)).astype(jnp.bfloat16)
    return np.stack([high, low])


def split(value):
    high = value.astype(jnp.bfloat16)
    low = (value - high.astype(jnp.float32)).astype(jnp.bfloat16)
    return high, low


def dot(a, b):
    return lax.dot_general(a, b, (((1,), (0,)), ((), ())), preferred_element_type=jnp.float32)


def dot3(a_high, a_low, b_high, b_low):
    rows = a_high.shape[0]
    both = dot(jnp.concatenate([a_high, a_low], axis=0), b_high)
    return both[:rows] + (both[rows:] + dot(a_high, b_low))


def mgrit_kernel(
    turns, shards, planes, chunks, behind, lags,
    guess, start, source, kernels_hbm, turned_hbm, rows_hbm, columns_hbm, out_ref,
    field, extra, kernels, turned, row_sines, column_sines, field_high, field_low, extra_high, extra_low,
    along, along_extra, gathered, spectra, begun, states, crossing, spread, returned, total,
    load_sem, kernel_sem, turned_sem, rows_sem, columns_sem, send_one, recv_one, send_extra, send_start,
    send_begun, recv_begun, send_cross, recv_cross, send_two, recv_two,
):
    tm, space = lax.axis_index("tm"), lax.axis_index("space")
    width = turns // planes
    group = width * shards
    last = planes - 1
    plane = tm // width
    place = lax.rem(tm, width)
    me = place * shards + space
    rows, length = field.shape
    half = length // 2
    tile = length // chunks
    deep = tile // group
    per_parity = chunks // 2
    has_guess = tm < turns - 2
    ahead = jnp.where(plane == last, behind[1], behind[0])
    wait_for = ahead + jnp.where(plane == last, lags[1], lags[0])
    join = 2 if chunks // 2 % 2 == 0 else 1

    field_load = pltpu.make_async_copy(guess.at[0], field, load_sem.at[0])
    field_load.start()
    kernel_load = pltpu.make_async_copy(kernels_hbm, kernels, kernel_sem)
    kernel_load.start()
    turned_load = pltpu.make_async_copy(turned_hbm, turned, turned_sem)
    turned_load.start()
    source_load = pltpu.make_async_copy(source, extra.at[pl.ds(0, rows), :], load_sem.at[1])
    source_load.start()
    start_load = pltpu.make_async_copy(start, extra.at[pl.ds(rows, rows), :], load_sem.at[2])
    start_load.start()
    columns_load = pltpu.make_async_copy(columns_hbm, column_sines, columns_sem)
    columns_load.start()

    def rows_load(chunk):
        return pltpu.make_async_copy(
            rows_hbm.at[pl.ds(pl.multiple_of(chunk * tile + me * deep, deep), deep), :],
            row_sines.at[pl.ds(pl.multiple_of(chunk * deep, deep), deep), :], rows_sem)

    for chunk in range(chunks):
        rows_load(chunk).start()

    def device(where, peer):
        return (where * width + peer // shards, lax.rem(peer, shards))

    def around(mine, count, act):
        def turn(step, carry):
            act(lax.rem(mine + step, count))
            return carry

        lax.fori_loop(1, count, turn, 0)

    barrier = pltpu.get_barrier_semaphore()

    def greet(who):
        pl.semaphore_signal(barrier, inc=1, device_id=who, device_id_type=MESH)

    around(me, group, lambda peer: greet(device(plane, peer)))

    @pl.when(plane > 0)
    def _():
        greet((tm - width, space))

    @pl.when(plane == 0)
    def _():
        greet((last * width + place, space))

    def rows_of(base, index):
        return pl.ds(pl.multiple_of(base + index * deep, deep), deep)

    def first_copy(chunk, peer):
        return pltpu.make_async_remote_copy(
            src_ref=along.at[rows_of(chunk * tile, peer), :],
            dst_ref=gathered.at[chunk, space, rows_of(0, place), :],
            send_sem=send_one, recv_sem=recv_one.at[chunk],
            device_id=device(plane, peer), device_id_type=MESH)

    def first_own(chunk):
        return pltpu.make_async_copy(
            along.at[rows_of(chunk * tile, me), :], gathered.at[chunk, space, rows_of(0, place), :],
            recv_one.at[chunk])

    def source_copy(chunk, shard):
        return pltpu.make_async_remote_copy(
            src_ref=along_extra.at[chunk, 0, rows_of(0, shard), :],
            dst_ref=gathered.at[chunk, space, pl.ds(width * deep, deep), :],
            send_sem=send_extra, recv_sem=recv_one.at[chunk],
            device_id=(tm, shard), device_id_type=MESH)

    def source_own(chunk):
        return pltpu.make_async_copy(
            along_extra.at[chunk, 0, rows_of(0, space), :], gathered.at[chunk, space, pl.ds(width * deep, deep), :],
            recv_one.at[chunk])

    def start_copy(chunk, shard):
        return pltpu.make_async_remote_copy(
            src_ref=along_extra.at[chunk, 1, rows_of(0, shard), :],
            dst_ref=gathered.at[chunk, space, pl.ds((width + 1) * deep, deep), :],
            send_sem=send_start, recv_sem=recv_one.at[chunk],
            device_id=(tm, shard), device_id_type=MESH)

    def start_own(chunk):
        return pltpu.make_async_copy(
            along_extra.at[chunk, 1, rows_of(0, space), :], gathered.at[chunk, space, pl.ds((width + 1) * deep, deep), :],
            recv_one.at[chunk])

    def begin_copy(chunk):
        return pltpu.make_async_remote_copy(
            src_ref=spectra.at[chunk, pl.ds((width + 1) * deep, deep), :], dst_ref=begun.at[chunk],
            send_sem=send_begun, recv_sem=recv_begun.at[chunk],
            device_id=(place, space), device_id_type=MESH)

    def cross_copy(chunk):
        return pltpu.make_async_remote_copy(
            src_ref=crossing.at[chunk], dst_ref=states.at[chunk, pl.ds(0, 2 * deep), :],
            send_sem=send_cross, recv_sem=recv_cross.at[chunk],
            device_id=(tm + width, space), device_id_type=MESH)

    def second_copy(chunk, peer):
        return pltpu.make_async_remote_copy(
            src_ref=spread.at[chunk, lax.rem(peer, shards), rows_of(0, peer // shards), :],
            dst_ref=returned.at[rows_of(chunk * tile, me), :],
            send_sem=send_two, recv_sem=recv_two.at[chunk],
            device_id=device(plane, peer), device_id_type=MESH)

    def second_own(chunk):
        return pltpu.make_async_copy(
            spread.at[chunk, space, rows_of(0, place), :], returned.at[rows_of(chunk * tile, me), :],
            recv_two.at[chunk])

    def arrived(ref, sem):
        pltpu.make_async_copy(ref, ref, sem).wait()

    def fold(value, high_ref, low_ref, columns):
        first, second = value[:, :half], value[:, half:]
        for which, part in enumerate((first + second, first - second)):
            high_ref[which, :, columns], low_ref[which, :, columns] = split(part.T)

    field_load.wait()
    fold(field[...], field_high, field_low, slice(0, rows))
    source_load.wait()
    fold(extra[:rows], extra_high, extra_low, slice(0, rows))
    start_load.wait()

    @pl.when(plane == last)
    def _():
        fold(extra[rows:], extra_high, extra_low, slice(rows, 2 * rows))

    kernel_load.wait()
    pl.semaphore_wait(
        barrier,
        group)

    def outward(chunk):
        which = chunk // per_parity
        offset = lax.rem(chunk, per_parity) * tile
        mine = pl.ds(pl.multiple_of(offset + place * (shards * deep), shards * deep), shards * deep)
        high, low = kernels[0, which, mine, :], kernels[1, which, mine, :]

        @pl.when(plane == last)
        def _():
            along_extra[chunk, 1] = dot3(high, low, extra_high[which, :, rows:], extra_low[which, :, rows:])
            start_own(chunk).start()
            around(space, shards, lambda shard: start_copy(chunk, shard).start())

        along_extra[chunk, 0] = dot3(high, low, extra_high[which, :, :rows], extra_low[which, :, :rows])
        source_own(chunk).start()
        around(space, shards, lambda shard: source_copy(chunk, shard).start())

        @pl.when(has_guess)
        def _():
            part = pl.ds(pl.multiple_of(offset, tile), tile)
            along[pl.ds(pl.multiple_of(chunk * tile, tile), tile), :] = dot3(
                kernels[0, which, part, :], kernels[1, which, part, :], field_high[which], field_low[which])
            first_own(chunk).start()
            around(me, group, lambda peer: first_copy(chunk, peer).start())

    arrived(row_sines, rows_sem)
    columns_load.wait()
    turned_load.wait()
    total[...] = jnp.zeros_like(total)

    lanes = 256
    across = length // lanes
    scale = 1.0 / float(length * length)
    steps = deep // 8 * across

    def mix(chunk, kind, index, carry):
        row = pl.multiple_of(index // across * 8, 8)
        lane = pl.ds(pl.multiple_of(lax.rem(index, across) * lanes, lanes), lanes)
        sines = row_sines[pl.ds(pl.multiple_of(chunk * deep + row, 8), 8), :]
        stiffness = 4.0 * (column_sines[:, lane] + jnp.concatenate([sines] * (lanes // 128), axis=1))
        fine_factor = 1.0 / (1.0 + decay_rate + spread_rate * stiffness)
        coarse = 1.0 / (1.0 + M * decay_rate + M * spread_rate * stiffness)
        fine, symbol, power = fine_factor, fine_factor, 1
        while power < M:
            symbol = symbol + fine * symbol
            fine = fine * fine
            power *= 2

        def at(turn):
            return pl.ds(pl.multiple_of(turn * deep + row, 8), 8)

        forcing = symbol * (scale * spectra[chunk, at(width), lane])
        gain = (fine * scale) * (fine - coarse)
        source_gain = (1.0 + fine - coarse) * forcing
        if kind == "first":
            state = fine * (scale * begun[chunk, pl.ds(row, 8), lane]) + forcing
            states[chunk, at(0), lane] = state
            state = fine * state + forcing
            states[chunk, at(1), lane] = state
        else:
            state = states[chunk, at(1), lane]
        for turn in range(2, width if kind == "last" else width + 2):
            state = coarse * state + (gain * spectra[chunk, at(turn - 2), lane] + source_gain)
            if turn < width:
                states[chunk, at(turn), lane] = state
            else:
                crossing[chunk, at(turn - width), lane] = state
        return carry

    def transform(chunk):
        @pl.when(plane == last)
        def _():
            arrived(gathered.at[chunk, :, pl.ds(0, width * deep), :], recv_one.at[chunk])

        @pl.when(plane < last)
        def _():
            arrived(gathered.at[chunk, :, pl.ds(0, (width + 1) * deep), :], recv_one.at[chunk])

        upper = [gathered[chunk, shard] for shard in range(shards // 2)]
        lower = [gathered[chunk, shard + shards // 2] for shard in range(shards // 2)]
        sums = [jnp.concatenate([a + b for a, b in zip(upper, lower)], axis=1)]
        sums.append(jnp.concatenate([a - b for a, b in zip(upper, lower)], axis=1))
        for which in range(2):
            right = (kernels[0, 0], kernels[1, 0]) if which == 0 else (turned[0], turned[1])
            spectra[chunk, :, which * half:(which + 1) * half] = dot3(*split(sums[which]), *right)

        @pl.when(plane == last)
        def _():
            begin_copy(chunk).start()

        @pl.when(plane == 0)
        def _():
            arrived(begun.at[chunk], recv_begun.at[chunk])
            lax.fori_loop(0, steps, functools.partial(mix, chunk, "first"), 0)
            cross_copy(chunk).start()

    def advance(chunk):
        @pl.when(plane > 0)
        def _():
            arrived(states.at[chunk, pl.ds(0, 2 * deep), :], recv_cross.at[chunk])

        @pl.when((plane > 0) & (plane < last))
        def _():
            lax.fori_loop(0, steps, functools.partial(mix, chunk, "middle"), 0)
            cross_copy(chunk).start()

        if width > 2:
            @pl.when(plane == last)
            def _():
                lax.fori_loop(0, steps, functools.partial(mix, chunk, "last"), 0)

        even_high, even_low = split(states[chunk, :, :half])
        odd_high, odd_low = split(states[chunk, :, half:])
        for shard in range(shards // 2):
            columns = slice(shard * rows, (shard + 1) * rows)
            even = dot3(even_high, even_low, kernels[0, 0, :, columns], kernels[1, 0, :, columns])
            odd = dot3(odd_high, odd_low, kernels[0, 1, :, columns], kernels[1, 1, :, columns])
            spread[chunk, shard] = even + odd
            spread[chunk, shard + shards // 2] = even - odd
        second_own(chunk).start()
        around(me, group, lambda peer: second_copy(chunk, peer).start())

    def inward(index, carry):
        block = pl.ds(pl.multiple_of(index * join * tile, join * tile), join * tile)
        for chunk in range(join):
            arrived(returned.at[pl.ds(0, tile), :], recv_two.at[index * join + chunk])
        which = index * join // per_parity
        part = pl.ds(pl.multiple_of(lax.rem(index * join, per_parity) * tile, join * tile), join * tile)
        high, low = split(returned[block, :].T)
        total[which] += dot3(high, low, kernels[0, which, part, :], kernels[1, which, part, :])
        return carry

    def step(time, carry):
        @pl.when(time < chunks)
        def _():
            outward(time)

        @pl.when((time >= ahead) & (time < ahead + chunks))
        def _():
            transform(time - ahead)

        @pl.when(time >= wait_for)
        def _():
            advance(time - wait_for)

        return carry

    lax.fori_loop(0, chunks + wait_for, step, 0)
    lax.fori_loop(0, chunks // join, inward, 0)
    out_ref[0, :, :half] = total[0] + total[1]
    out_ref[0, :, half:] = total[0] - total[1]

    @pl.when(has_guess)
    def _():
        arrived(along.at[pl.ds(0, (group - 1) * deep * chunks), :], send_one)

    arrived(along_extra.at[:, 0, pl.ds(0, (shards - 1) * deep), :], send_extra)

    @pl.when(plane == last)
    def _():
        arrived(along_extra.at[:, 1, pl.ds(0, (shards - 1) * deep), :], send_start)
        arrived(begun, send_begun)

    @pl.when(plane < last)
    def _():
        arrived(crossing, send_cross)

    arrived(along.at[pl.ds(0, (group - 1) * deep * chunks), :], send_two)


def body(turns, shards, initial_guess, start_field, source_field):
    rows, length = start_field.shape
    planes = 2
    width = turns // planes
    group = width * shards
    half = length // 2
    chunks = min(8, length // group // 8)
    tile = length // chunks
    deep = tile // group
    halves = half_kernels(length)
    kernels = jnp.asarray(halves)
    turned = jnp.asarray(np.ascontiguousarray(halves[:, 1].transpose(0, 2, 1)))
    sines = (np.sin(np.pi * mode_order(length) / length) ** 2).astype(np.float32)
    row_sines = jnp.asarray(np.repeat(sines[:, None], 128, axis=1))
    column_sines = jnp.asarray(np.repeat(sines[None, :], 8, axis=0))
    f32, bf16 = jnp.float32, jnp.bfloat16
    dma = pltpu.SemaphoreType.DMA
    return pl.pallas_call(
        functools.partial(mgrit_kernel, turns, shards, planes, chunks, (5, 3), (2, 5)),
        out_shape=jax.ShapeDtypeStruct(initial_guess.shape, f32),
        in_specs=[pl.BlockSpec(memory_space=pltpu.HBM)] * 7,
        out_specs=pl.BlockSpec(memory_space=pltpu.VMEM),
        scratch_shapes=[
            pltpu.VMEM((rows, length), f32),
            pltpu.VMEM((2 * rows, length), f32),
            pltpu.VMEM((2, 2, half, half), bf16),
            pltpu.VMEM((2, half, half), bf16),
            pltpu.VMEM((chunks * deep, 128), f32),
            pltpu.VMEM((8, length), f32),
            pltpu.VMEM((2, half, rows), bf16),
            pltpu.VMEM((2, half, rows), bf16),
            pltpu.VMEM((2, half, 2 * rows), bf16),
            pltpu.VMEM((2, half, 2 * rows), bf16),
            pltpu.VMEM((length, rows), f32),
            pltpu.VMEM((chunks, 2, shards * deep, rows), f32),
            pltpu.VMEM((chunks, shards, (width + 2) * deep, rows), f32),
            pltpu.VMEM((chunks, (width + 2) * deep, length), f32),
            pltpu.VMEM((chunks, deep, length), f32),
            pltpu.VMEM((chunks, width * deep, length), f32),
            pltpu.VMEM((chunks, 2 * deep, length), f32),
            pltpu.VMEM((chunks, shards, width * deep, rows), f32),
            pltpu.VMEM((length, rows), f32),
            pltpu.VMEM((2, rows, half), f32),
            dma((3,)), dma, dma, dma, dma, dma, dma((chunks,)), dma, dma,
            dma, dma((chunks,)), dma, dma((chunks,)), dma, dma((chunks,)),
        ],
        compiler_params=pltpu.CompilerParams(
            collective_id=0, has_side_effects=True, vmem_limit_bytes=40 * 1024 * 1024),
    )(*(pltpu.with_memory_space_constraint(value, pltpu.HBM)
        for value in (initial_guess, start_field, source_field, kernels, turned, row_sines, column_sines)))


def solution(mesh):
    return jax.shard_map(
        functools.partial(body, mesh.shape["tm"], mesh.shape["space"]),
        mesh=mesh,
        in_specs=(P("tm", "space", None), P("space", None), P("space", None)),
        out_specs=P("tm", "space", None),
        check_vma=False,
    )
```

```python
import functools

import jax
import jax.numpy as jnp
import numpy as np
from jax import lax
from jax.experimental import pallas as pl
from jax.experimental.pallas import tpu as pltpu
from jax.sharding import PartitionSpec as P

M = 16
MESH = pl.DeviceIdType.MESH

decay_rate = 0.0005
spread_rate = 0.01


def mode_order(length):
    return np.concatenate([np.arange(0, length, 2), np.arange(1, length, 2)])


def half_kernels(length):
    half = length // 2
    product = mode_order(length)[:, None] * np.arange(half)[None, :] % length
    angles = 2.0 * np.pi / length * product
    full = (np.cos(angles) + np.sin(angles)).astype(np.float32).reshape(2, half, half)
    high = full.astype(jnp.bfloat16)
    low = (full - high.astype(np.float32)).astype(jnp.bfloat16)
    return np.stack([high, low])


def split(value):
    high = value.astype(jnp.bfloat16)
    low = (value - high.astype(jnp.float32)).astype(jnp.bfloat16)
    return high, low


def dot(a, b):
    return lax.dot_general(a, b, (((1,), (0,)), ((), ())), preferred_element_type=jnp.float32)


def dot3(a_high, a_low, b_high, b_low):
    rows = a_high.shape[0]
    both = dot(jnp.concatenate([a_high, a_low], axis=0), b_high)
    return both[:rows] + (both[rows:] + dot(a_high, b_low))


def mgrit_kernel(
    turns, shards, planes, chunks, behind, lags,
    guess, start, source, kernels_hbm, turned_hbm, rows_hbm, columns_hbm, out_ref,
    field, extra, kernels, turned, row_sines, column_sines, field_high, field_low, extra_high, extra_low,
    along, along_extra, gathered, spectra, begun, states, crossing, spread, returned, total,
    load_sem, kernel_sem, turned_sem, rows_sem, columns_sem, send_one, recv_one, send_extra, send_start,
    send_begun, recv_begun, send_cross, recv_cross, send_two, recv_two,
):
    tm, space = lax.axis_index("tm"), lax.axis_index("space")
    width = turns // planes
    group = width * shards
    last = planes - 1
    plane = tm // width
    place = lax.rem(tm, width)
    me = place * shards + space
    rows, length = field.shape
    half = length // 2
    tile = length // chunks
    deep = tile // group
    per_parity = chunks // 2
    has_guess = tm < turns - 2
    ahead = jnp.where(plane == last, behind[1], behind[0])
    wait_for = ahead + jnp.where(plane == last, lags[1], lags[0])
    join = 2 if chunks // 2 % 2 == 0 else 1

    field_load = pltpu.make_async_copy(guess.at[0], field, load_sem.at[0])
    field_load.start()
    kernel_loads = [
        pltpu.make_async_copy(kernels_hbm.at[:, which], kernels.at[:, which], kernel_sem.at[which]) for which in range(2)]
    kernel_loads[0].start()
    source_load = pltpu.make_async_copy(source, extra.at[pl.ds(0, rows), :], load_sem.at[1])
    source_load.start()
    start_load = pltpu.make_async_copy(start, extra.at[pl.ds(rows, rows), :], load_sem.at[2])

    @pl.when(plane == last)
    def _():
        start_load.start()

    kernel_loads[1].start()
    turned_load = pltpu.make_async_copy(turned_hbm, turned, turned_sem)
    turned_load.start()
    columns_load = pltpu.make_async_copy(columns_hbm, column_sines, columns_sem)
    columns_load.start()

    def rows_load(chunk):
        return pltpu.make_async_copy(
            rows_hbm.at[pl.ds(pl.multiple_of(chunk * tile + me * deep, deep), deep), :],
            row_sines.at[pl.ds(pl.multiple_of(chunk * deep, deep), deep), :], rows_sem)

    for chunk in range(chunks):
        rows_load(chunk).start()

    def device(where, peer):
        return (where * width + peer // shards, lax.rem(peer, shards))

    def around(mine, count, act):
        def turn(step, carry):
            act(lax.rem(mine + step, count))
            return carry

        lax.fori_loop(1, count, turn, 0)

    bits = [1 << k for k in range(group.bit_length() - 1)]
    moves = [bit - 2 * bit * lax.rem(me // bit, 2) for bit in bits]

    def paired(act):
        for mask in range(group - 1, 0, -1):
            act(me + sum(move for bit, move in zip(bits, moves) if mask & bit))

    barrier = pltpu.get_barrier_semaphore()

    def greet(who):
        pl.semaphore_signal(barrier, inc=1, device_id=who, device_id_type=MESH)

    around(me, group, lambda peer: greet(device(plane, peer)))

    @pl.when(plane > 0)
    def _():
        greet((tm - width, space))

    @pl.when(plane == 0)
    def _():
        greet((last * width + place, space))

    def rows_of(base, index):
        return pl.ds(pl.multiple_of(base + index * deep, deep), deep)

    def first_copy(chunk, peer):
        return pltpu.make_async_remote_copy(
            src_ref=along.at[rows_of(chunk * tile, peer), :],
            dst_ref=gathered.at[chunk, space, rows_of(0, place), :],
            send_sem=send_one, recv_sem=recv_one.at[chunk],
            device_id=device(plane, peer), device_id_type=MESH)

    def first_own(chunk):
        return pltpu.make_async_copy(
            along.at[rows_of(chunk * tile, me), :], gathered.at[chunk, space, rows_of(0, place), :],
            recv_one.at[chunk])

    def source_copy(chunk, shard):
        return pltpu.make_async_remote_copy(
            src_ref=along_extra.at[chunk, 0, rows_of(0, shard), :],
            dst_ref=gathered.at[chunk, space, pl.ds(width * deep, deep), :],
            send_sem=send_extra, recv_sem=recv_one.at[chunk],
            device_id=(tm, shard), device_id_type=MESH)

    def source_own(chunk):
        return pltpu.make_async_copy(
            along_extra.at[chunk, 0, rows_of(0, space), :], gathered.at[chunk, space, pl.ds(width * deep, deep), :],
            recv_one.at[chunk])

    def start_copy(chunk, shard):
        return pltpu.make_async_remote_copy(
            src_ref=along_extra.at[chunk, 1, rows_of(0, shard), :],
            dst_ref=gathered.at[chunk, space, pl.ds((width + 1) * deep, deep), :],
            send_sem=send_start, recv_sem=recv_one.at[chunk],
            device_id=(tm, shard), device_id_type=MESH)

    def start_own(chunk):
        return pltpu.make_async_copy(
            along_extra.at[chunk, 1, rows_of(0, space), :], gathered.at[chunk, space, pl.ds((width + 1) * deep, deep), :],
            recv_one.at[chunk])

    def begin_copy(chunk):
        return pltpu.make_async_remote_copy(
            src_ref=spectra.at[chunk, pl.ds((width + 1) * deep, deep), :], dst_ref=begun.at[chunk],
            send_sem=send_begun, recv_sem=recv_begun.at[chunk],
            device_id=(place, space), device_id_type=MESH)

    def cross_copy(chunk):
        return pltpu.make_async_remote_copy(
            src_ref=crossing.at[chunk], dst_ref=states.at[chunk, pl.ds(0, 2 * deep), :],
            send_sem=send_cross, recv_sem=recv_cross.at[chunk],
            device_id=(tm + width, space), device_id_type=MESH)

    def second_copy(chunk, peer):
        return pltpu.make_async_remote_copy(
            src_ref=spread.at[chunk, lax.rem(peer, shards), rows_of(0, peer // shards), :],
            dst_ref=returned.at[rows_of(chunk * tile, me), :],
            send_sem=send_two, recv_sem=recv_two.at[chunk],
            device_id=device(plane, peer), device_id_type=MESH)

    def second_own(chunk):
        return pltpu.make_async_copy(
            spread.at[chunk, space, rows_of(0, place), :], returned.at[rows_of(chunk * tile, me), :],
            recv_two.at[chunk])

    def arrived(ref, sem):
        pltpu.make_async_copy(ref, ref, sem).wait()

    def fold(value, high_ref, low_ref, columns):
        first, second = value[:, :half], value[:, half:]
        for which, part in enumerate((first + second, first - second)):
            high_ref[which, :, columns], low_ref[which, :, columns] = split(part.T)

    field_load.wait()
    fold(field[...], field_high, field_low, slice(0, rows))
    source_load.wait()
    fold(extra[:rows], extra_high, extra_low, slice(0, rows))

    @pl.when(plane == last)
    def _():
        start_load.wait()
        fold(extra[rows:], extra_high, extra_low, slice(rows, 2 * rows))

    kernel_loads[0].wait()
    pl.semaphore_wait(
        barrier,
        group)

    def outward(chunk):
        which = chunk // per_parity
        offset = lax.rem(chunk, per_parity) * tile
        mine = pl.ds(pl.multiple_of(offset + place * (shards * deep), shards * deep), shards * deep)
        high, low = kernels[0, which, mine, :], kernels[1, which, mine, :]

        @pl.when(plane == last)
        def _():
            along_extra[chunk, 1] = dot3(high, low, extra_high[which, :, rows:], extra_low[which, :, rows:])
            start_own(chunk).start()
            around(space, shards, lambda shard: start_copy(chunk, shard).start())

        along_extra[chunk, 0] = dot3(high, low, extra_high[which, :, :rows], extra_low[which, :, :rows])
        source_own(chunk).start()
        around(space, shards, lambda shard: source_copy(chunk, shard).start())

        @pl.when(has_guess)
        def _():
            part = pl.ds(pl.multiple_of(offset, tile), tile)
            along[pl.ds(pl.multiple_of(chunk * tile, tile), tile), :] = dot3(
                kernels[0, which, part, :], kernels[1, which, part, :], field_high[which], field_low[which])
            first_own(chunk).start()
            paired(lambda peer: first_copy(chunk, peer).start())

    arrived(row_sines, rows_sem)
    columns_load.wait()
    total[...] = jnp.zeros_like(total)

    lanes = 512
    across = length // lanes
    scale = 1.0 / float(length * length)
    steps = deep // 8 * across

    def mix(chunk, kind, index, carry):
        row = pl.multiple_of(index // across * 8, 8)
        lane = pl.ds(pl.multiple_of(lax.rem(index, across) * lanes, lanes), lanes)
        sines = row_sines[pl.ds(pl.multiple_of(chunk * deep + row, 8), 8), :]
        stiffness = 4.0 * (column_sines[:, lane] + jnp.concatenate([sines] * (lanes // 128), axis=1))
        fine_factor = 1.0 / (1.0 + decay_rate + spread_rate * stiffness)
        coarse = 1.0 / (1.0 + M * decay_rate + M * spread_rate * stiffness)
        fine, symbol, power = fine_factor, fine_factor, 1
        while power < M:
            symbol = symbol + fine * symbol
            fine = fine * fine
            power *= 2

        def at(turn):
            return pl.ds(pl.multiple_of(turn * deep + row, 8), 8)

        forcing = symbol * (scale * spectra[chunk, at(width), lane])
        gain = (fine * scale) * (fine - coarse)
        source_gain = (1.0 + fine - coarse) * forcing
        if kind == "first":
            state = fine * (scale * begun[chunk, pl.ds(row, 8), lane]) + forcing
            states[chunk, at(0), lane] = state
            state = fine * state + forcing
            states[chunk, at(1), lane] = state
        else:
            state = states[chunk, at(1), lane]
        for turn in range(2, width if kind == "last" else width + 2):
            state = coarse * state + (gain * spectra[chunk, at(turn - 2), lane] + source_gain)
            if turn < width:
                states[chunk, at(turn), lane] = state
            else:
                crossing[chunk, at(turn - width), lane] = state
        return carry

    def transform(chunk):
        @pl.when(plane == last)
        def _():
            arrived(gathered.at[chunk, :, pl.ds(0, width * deep), :], recv_one.at[chunk])

        @pl.when(plane < last)
        def _():
            arrived(gathered.at[chunk, :, pl.ds(0, (width + 1) * deep), :], recv_one.at[chunk])

        upper = [gathered[chunk, shard] for shard in range(shards // 2)]
        lower = [gathered[chunk, shard + shards // 2] for shard in range(shards // 2)]
        sums = [jnp.concatenate([a + b for a, b in zip(upper, lower)], axis=1)]
        sums.append(jnp.concatenate([a - b for a, b in zip(upper, lower)], axis=1))
        for which in range(2):
            right = (kernels[0, 0], kernels[1, 0]) if which == 0 else (turned[0], turned[1])
            spectra[chunk, :, which * half:(which + 1) * half] = dot3(*split(sums[which]), *right)

        @pl.when(plane == last)
        def _():
            begin_copy(chunk).start()

        @pl.when(plane == 0)
        def _():
            arrived(begun.at[chunk], recv_begun.at[chunk])
            lax.fori_loop(0, steps, functools.partial(mix, chunk, "first"), 0)
            cross_copy(chunk).start()

    def advance(chunk):
        @pl.when(plane > 0)
        def _():
            arrived(states.at[chunk, pl.ds(0, 2 * deep), :], recv_cross.at[chunk])

        @pl.when((plane > 0) & (plane < last))
        def _():
            lax.fori_loop(0, steps, functools.partial(mix, chunk, "middle"), 0)
            cross_copy(chunk).start()

        if width > 2:
            @pl.when(plane == last)
            def _():
                lax.fori_loop(0, steps, functools.partial(mix, chunk, "last"), 0)

        even_high, even_low = split(states[chunk, :, :half])
        odd_high, odd_low = split(states[chunk, :, half:])
        for shard in range(shards // 2):
            columns = slice(shard * rows, (shard + 1) * rows)
            even = dot3(even_high, even_low, kernels[0, 0, :, columns], kernels[1, 0, :, columns])
            odd = dot3(odd_high, odd_low, kernels[0, 1, :, columns], kernels[1, 1, :, columns])
            spread[chunk, shard] = even + odd
            spread[chunk, shard + shards // 2] = even - odd
        second_own(chunk).start()
        paired(lambda peer: second_copy(chunk, peer).start())

    def inward(index, carry):
        block = pl.ds(pl.multiple_of(index * join * tile, join * tile), join * tile)
        for chunk in range(join):
            arrived(returned.at[pl.ds(0, tile), :], recv_two.at[index * join + chunk])
        which = index * join // per_parity
        part = pl.ds(pl.multiple_of(lax.rem(index * join, per_parity) * tile, join * tile), join * tile)
        high, low = split(returned[block, :].T)
        total[which] += dot3(high, low, kernels[0, which, part, :], kernels[1, which, part, :])
        return carry

    def step(time, carry):
        @pl.when(time == 1)
        def _():
            kernel_loads[1].wait()
            turned_load.wait()

        @pl.when(time < chunks)
        def _():
            outward(time)

        @pl.when((time >= ahead) & (time < ahead + chunks))
        def _():
            transform(time - ahead)

        @pl.when(time >= wait_for)
        def _():
            advance(time - wait_for)

        return carry

    lax.fori_loop(0, chunks + wait_for, step, 0)
    lax.fori_loop(0, chunks // join, inward, 0)
    out_ref[0, :, :half] = total[0] + total[1]
    out_ref[0, :, half:] = total[0] - total[1]

    @pl.when(has_guess)
    def _():
        arrived(along.at[pl.ds(0, (group - 1) * deep * chunks), :], send_one)

    arrived(along_extra.at[:, 0, pl.ds(0, (shards - 1) * deep), :], send_extra)

    @pl.when(plane == last)
    def _():
        arrived(along_extra.at[:, 1, pl.ds(0, (shards - 1) * deep), :], send_start)
        arrived(begun, send_begun)

    @pl.when(plane < last)
    def _():
        arrived(crossing, send_cross)

    arrived(along.at[pl.ds(0, (group - 1) * deep * chunks), :], send_two)


def body(turns, shards, initial_guess, start_field, source_field):
    rows, length = start_field.shape
    planes = 2
    width = turns // planes
    group = width * shards
    half = length // 2
    chunks = min(8, length // group // 8)
    tile = length // chunks
    deep = tile // group
    halves = half_kernels(length)
    kernels = jnp.asarray(halves)
    turned = jnp.asarray(np.ascontiguousarray(halves[:, 1].transpose(0, 2, 1)))
    sines = (np.sin(np.pi * mode_order(length) / length) ** 2).astype(np.float32)
    row_sines = jnp.asarray(np.repeat(sines[:, None], 128, axis=1))
    column_sines = jnp.asarray(np.repeat(sines[None, :], 8, axis=0))
    f32, bf16 = jnp.float32, jnp.bfloat16
    dma = pltpu.SemaphoreType.DMA
    return pl.pallas_call(
        functools.partial(mgrit_kernel, turns, shards, planes, chunks, (5, 3), (2, 5)),
        out_shape=jax.ShapeDtypeStruct(initial_guess.shape, f32),
        in_specs=[pl.BlockSpec(memory_space=pltpu.HBM)] * 7,
        out_specs=pl.BlockSpec(memory_space=pltpu.VMEM),
        scratch_shapes=[
            pltpu.VMEM((rows, length), f32),
            pltpu.VMEM((2 * rows, length), f32),
            pltpu.VMEM((2, 2, half, half), bf16),
            pltpu.VMEM((2, half, half), bf16),
            pltpu.VMEM((chunks * deep, 128), f32),
            pltpu.VMEM((8, length), f32),
            pltpu.VMEM((2, half, rows), bf16),
            pltpu.VMEM((2, half, rows), bf16),
            pltpu.VMEM((2, half, 2 * rows), bf16),
            pltpu.VMEM((2, half, 2 * rows), bf16),
            pltpu.VMEM((length, rows), f32),
            pltpu.VMEM((chunks, 2, shards * deep, rows), f32),
            pltpu.VMEM((chunks, shards, (width + 2) * deep, rows), f32),
            pltpu.VMEM((chunks, (width + 2) * deep, length), f32),
            pltpu.VMEM((chunks, deep, length), f32),
            pltpu.VMEM((chunks, width * deep, length), f32),
            pltpu.VMEM((chunks, 2 * deep, length), f32),
            pltpu.VMEM((chunks, shards, width * deep, rows), f32),
            pltpu.VMEM((length, rows), f32),
            pltpu.VMEM((2, rows, half), f32),
            dma((3,)), dma((2,)), dma, dma, dma, dma, dma((chunks,)), dma, dma,
            dma, dma((chunks,)), dma, dma((chunks,)), dma, dma((chunks,)),
        ],
        compiler_params=pltpu.CompilerParams(
            collective_id=0, has_side_effects=True, vmem_limit_bytes=40 * 1024 * 1024),
    )(*(pltpu.with_memory_space_constraint(value, pltpu.HBM)
        for value in (initial_guess, start_field, source_field, kernels, turned, row_sines, column_sines)))


def solution(mesh):
    return jax.shard_map(
        functools.partial(body, mesh.shape["tm"], mesh.shape["space"]),
        mesh=mesh,
        in_specs=(P("tm", "space", None), P("space", None), P("space", None)),
        out_specs=P("tm", "space", None),
        check_vma=False,
    )
```
